32 devices in a mesh: segment: 4 (over y, x), col: 8 (over z, core).
Axes of the slice: x: 2, y: 2, z: 4, core: 2. Of those that a mesh axis runs over, the one named last changes fastest.
Arguments:
- left_env: bfloat16 [384, 8192], P(None, 'col'), may hold values from -6 to 6
- bit_strings: int32 [384, 4], P(None, 'segment'), may hold values from 0 to 1
- site_tensors: bfloat16 [4, 2, 8192, 8192], P('segment', None, None, 'col'), may hold values from -0.0625 to 0.0625
Outputs:
- section_env: bfloat16 [4, 384, 8192], P('segment', None, 'col')
- section_log: float32 [4, 384], P('segment')
The draws below stay inside these ranges and needn't reach their ends.
All inputs are finite; a program needn't handle non-finite values. Where the reference program divides by a largest or mean magnitude, that divisor is 1e-20 or more.
Results may differ from the reference program's by a relative error of at most 0.0065.
Values may be sent and summed in bfloat16 or wider, within the bound.
A program may use at most 128 MiB of HBM per device.

```python
import jax
import jax.numpy as jnp
from jax import lax

CHI = 8192
PHYS = 2
ROWS = 384
SITES_SEGMENT = 1
SECTIONS = 4
SITES = 4


def touch_ends(array, key, smallest, largest):
    spot = [jax.random.randint(jax.random.fold_in(key, axis), (), 0, length) for axis, length in enumerate(array.shape)]
    main_axis = array.shape.index(max(array.shape))
    neighbour = spot[:main_axis] + [(spot[main_axis] + 1) % array.shape[main_axis]] + spot[main_axis + 1:]
    return array.at[tuple(spot)].set(smallest).at[tuple(neighbour)].set(largest)


def steps_of(stream_key, dims, cuts, low, largest):
    gain = 1.0
    for dim, blocks in cuts:
        steps = jax.random.uniform(jax.random.fold_in(jax.random.fold_in(stream_key, 6), dim), (blocks,), jnp.float32, low / len(cuts), largest / len(cuts))
        gain = gain * jnp.repeat(jnp.exp(steps), dims[dim] // blocks).reshape((-1,) + (1,) * (len(dims) - 1 - dim))
    return gain


def bell_draw(key, dims, scale, limit, shards=(), held_as=jnp.bfloat16):
    result = jax.random.normal(key, dims, jnp.float32) * scale
    if len(shards) > 0:
        result = steps_of(key, dims, shards, -0.22, 0.18) * result
    return jnp.clip(result, min=-limit, max=limit).astype(held_as)


def setup_inputs(seed: int = 0) -> dict:
    streams_of = jax.random.split(jax.random.key(seed), 4)
    left_env = bell_draw(streams_of[0], (ROWS, CHI), 1.0, 6.0, ((1, 8),))
    bit_strings = touch_ends(jax.random.randint(streams_of[1], (ROWS, SITES), 0, 2), jax.random.fold_in(streams_of[1], 1), 0, 1).astype(jnp.int32)
    site_tensors = bell_draw(streams_of[2], (SITES, PHYS, CHI, CHI), CHI ** -0.5, 0.0625, ((0, 4), (3, 8)))
    return dict(left_env=left_env, bit_strings=bit_strings, site_tensors=site_tensors)


def reference(left_env, bit_strings, site_tensors):
    vector = left_env
    env_list = []
    log_list = []
    for section in range(SECTIONS):
        log_total = jnp.zeros((ROWS,), jnp.float32)
        for inner in range(SITES_SEGMENT):
            site_index = section * SITES_SEGMENT + inner
            operand = vector.astype(jnp.float32)
            product_zero = jnp.dot(operand, site_tensors[site_index, 0].astype(jnp.float32), precision=lax.Precision.HIGHEST)
            product_one = jnp.dot(operand, site_tensors[site_index, 1].astype(jnp.float32), precision=lax.Precision.HIGHEST)
            chosen = jnp.where(bit_strings[:, site_index:site_index + 1] == 1, product_one, product_zero)
            maximum = jnp.max(jnp.abs(chosen), axis=1) + jnp.float32(1e-6)
            vector = (chosen / maximum[:, None]).astype(jnp.bfloat16)
            log_total = log_total + jnp.log(maximum)
        env_list.append(vector)
        log_list.append(log_total)
    return jnp.stack(env_list), jnp.stack(log_list)
```

```python
import functools

import jax
import jax.numpy as jnp
from jax import lax
from jax.experimental import pallas as pl
from jax.experimental.pallas import tpu as pltpu
from jax.sharding import PartitionSpec as P

EPSILON = 1e-06
REACH = (0, 2, -2, 1, -1)
MESH = pl.DeviceIdType.MESH
UNIT = 16
BLOCK = 48


def block_of(rows):
    for block in range(BLOCK, 0, -UNIT):
        if rows % block == 0:
            return block
    return rows


def chip_at(step, z, n):
    low = jnp.where(step <= n - 1 - z, z + step, n - 1 - step)
    high = jnp.where(step <= z, z - step, step)
    return jnp.where(2 * z < n, low, high)


def kernel(
    stages, peers, block,
    env_in, bits_in, tensor_in, env_out, log_out,
    weights, pieces, product, outgoing, peak, peak_sent, peak_all, scale_in, scale_sent,
    load_sem, weight_sem, arrive_sem, line_sem, cross_sem, next_sem,
    peak_send_sem, peak_recv_sem, scale_send_sem, scale_recv_sem, env_sem, first_sem, env_all,
):
    rows, width = outgoing.shape
    granules = rows // block
    n = peers // 2
    stage = lax.axis_index("segment")
    me = lax.axis_index("col")
    z = me // 2
    core = me % 2

    def there(segment, col):
        return {"segment": segment, "col": col}

    load = pltpu.make_async_copy(env_in, env_all, load_sem.at[0])
    keep = pltpu.make_async_copy(env_in, pieces.at[me], load_sem.at[1])
    load.start()

    @pl.when(stage == 0)
    def _():
        keep.start()

    def owner_at(step):
        return chip_at(step // 2, z, n) * 2 + (core + step) % 2

    def weight_copy(owner):
        return pltpu.make_async_copy(
            tensor_in.at[0, :, pl.ds(pl.multiple_of(owner * width, width), width), :],
            weights.at[owner],
            weight_sem.at[owner],
        )

    def start_weight(step, carry):
        weight_copy(owner_at(step)).start()
        return carry

    lax.fori_loop(0, peers, start_weight, 0)

    barrier = pltpu.get_barrier_semaphore()

    def greet(by, carry):
        pl.semaphore_signal(
            barrier, inc=1, device_id=there(stage, (me + by) % peers), device_id_type=MESH
        )
        return carry

    lax.fori_loop(1, peers, greet, 0)

    def meet(turn, carry):
        segment = (stage + 1 + turn // n) % stages
        col = (z + turn) % n * 2 + core
        pl.semaphore_signal(barrier, inc=1, device_id=there(segment, col), device_id_type=MESH)
        return carry

    lax.fori_loop(0, (stages - 1) * n, meet, 0)
    pl.semaphore_wait(barrier, peers - 1 + (stages - 1) * n)

    load.wait()

    @pl.when(stage == 0)
    def _():
        keep.wait()

    def rows_of(granule):
        return pl.ds(pl.multiple_of(granule * block, block), block)

    def send(source, granule, owner, sem, segment, col):
        return pltpu.make_async_remote_copy(
            src_ref=source,
            dst_ref=pieces.at[owner, rows_of(granule), :],
            send_sem=sem,
            recv_sem=arrive_sem.at[granule, owner],
            device_id=there(segment, col),
            device_id_type=MESH,
        )

    def piece(granule, owner):
        return pieces.at[owner, rows_of(granule), :]

    def cross(granule, owner):
        sem = cross_sem.at[granule, owner // 2]
        return send(piece(granule, owner), granule, owner, sem, stage, 2 * z + 1 - core)

    end = (z == 0) | (z == n - 1)

    def spread(act, source, granule, segment, sems, slots):
        for slot in slots:
            by = REACH[slot]
            goes = (z + by >= 0) & (z + by < n)
            if by in (-1, 1):
                goes = goes & jnp.logical_not(end)

            @pl.when(goes)
            def _():
                act(send(source, granule, me, sems.at[slot, granule], segment, me + 2 * by))

    def supply_first(act):
        def supply_chip(by, carry):
            chip = (z + by) % n
            near = jnp.abs(chip - z) == 1

            @pl.when(stage == jnp.where(near, 0, 1))
            def _():
                source = env_all.at[rows_of(0), :]
                act(send(source, 0, me, first_sem.at[by], 0, chip * 2 + core))

            return carry

        lax.fori_loop(1, n, supply_chip, 0)

    def supply(act, granule):
        @pl.when(stage == jnp.minimum(granule + 1, stages - 1))
        def _():
            source = env_all.at[rows_of(granule), :]
            spread(act, source, granule, 0, env_sem, range(1, len(REACH)))

    def onward(act, granule):
        @pl.when(stage < stages - 1)
        def _():
            source = outgoing.at[rows_of(granule), :]
            spread(act, source, granule, stage + 1, next_sem, range(len(REACH)))

    def relays(granule, chip):
        needed = (stage > 0) | (granule > 0)
        return needed & (z != chip) & ((z - chip) % 2 == 0)

    def along(act, granule, chip):
        owner = chip * 2 + core
        source = piece(granule, owner)
        for slot, by in enumerate((1, -1, 2, -2)):
            goes = relays(granule, chip) & ((chip < z) if by > 0 else (chip > z))
            if by in (-1, 1):
                goes = goes | (((stage > 0) | (granule > 0)) & end & (chip == z))

            @pl.when(goes & (z + by >= 0) & (z + by < n))
            def _():
                sem = line_sem.at[slot, granule, chip]
                act(send(source, granule, owner, sem, stage, me + 2 * by))

    def start(copy):
        copy.start()

    def sent(copy):
        copy.wait_send()

    def open_granule(granule):
        @pl.when(stage > 0)
        def _():
            cross(granule, me).wait_recv()

        along(start, granule, z)
        cross(granule, me).start()

    def supply_one(granule, carry):
        supply(start, granule)
        return carry

    supply_first(start)
    lax.fori_loop(1, granules, supply_one, 0)
    chips = [chip_at(step, z, n) for step in range(n)]

    open_granule(0)

    def one_granule(granule, carry):
        here = rows_of(granule)
        bit = bits_in[here, :] == 1

        def take(chip):
            cross(granule, chip * 2 + core).wait_recv()
            along(start, granule, chip)
            cross(granule, chip * 2 + core).start()

        def add(owners, first=False):
            @pl.when(granule == 0)
            def _():
                for owner in owners:
                    weight_copy(owner).wait()

            def against(which):
                total = None
                for owner in owners:
                    one = jnp.dot(
                        piece(granule, owner)[...],
                        weights[owner, which],
                        preferred_element_type=jnp.float32,
                    )
                    total = one if total is None else total + one
                return total

            part = jnp.where(bit, against(1), against(0))
            if first:
                product[here, :] = part
            else:
                product[here, :] += part

        def others(step):
            other = chips[step] * 2 + 1 - core
            cross(granule, other).wait_recv()
            return other

        for step, chip in enumerate(chips):
            own = chip * 2 + core
            last = step == n - 1
            if last:

                @pl.when(granule + 1 < granules)
                def _():
                    open_granule(granule + 1)

            if step > 0:

                @pl.when(relays(granule, chip))
                def _():
                    take(chip)

                if last:
                    add([others(step - 1)])

                @pl.when(jnp.logical_not(relays(granule, chip)))
                def _():
                    take(chip)

            if step == 0 or last:
                add([own], first=step == 0)
            else:
                add([others(step - 1), own])
        add([others(n - 1)])

        done = product[here, :]
        outgoing[here, :] = done.astype(jnp.bfloat16)
        onward(start, granule)
        largest = jnp.max(jnp.abs(done), axis=1, keepdims=True)
        peak[here, :] = jnp.broadcast_to(largest, (block, peak.shape[1]))
        return carry

    lax.fori_loop(0, granules, one_granule, 0)

    mine = jnp.transpose(peak[...])[:8]
    peak_sent[...] = mine

    def peak_copy(by):
        return pltpu.make_async_remote_copy(
            src_ref=peak_sent,
            dst_ref=peak_all.at[by],
            send_sem=peak_send_sem.at[by],
            recv_sem=peak_recv_sem.at[by],
            device_id=there(stage, (me + by) % peers),
            device_id_type=MESH,
        )

    def start_peak(by, carry):
        peak_copy(by).start()
        return carry

    lax.fori_loop(1, peers, start_peak, 0)

    def drain(granule, carry):
        def drain_chip(chip, carry):
            along(sent, granule, chip)
            cross(granule, chip * 2 + core).wait_send()
            return carry

        lax.fori_loop(0, n, drain_chip, 0)
        onward(sent, granule)
        return carry

    lax.fori_loop(0, granules, drain, 0)

    def supplied(granule, carry):
        supply(sent, granule)
        return carry

    supply_first(sent)
    lax.fori_loop(1, granules, supplied, 0)

    scale_copy = pltpu.make_async_remote_copy(
        src_ref=scale_sent,
        dst_ref=scale_in,
        send_sem=scale_send_sem,
        recv_sem=scale_recv_sem,
        device_id=there(stage + 1, me),
        device_id_type=MESH,
    )

    @pl.when(stage == 0)
    def _():
        scale_in[...] = jnp.ones_like(scale_in)

    @pl.when(stage > 0)
    def _():
        scale_copy.wait_recv()

    def take_peak(by, largest):
        peak_copy(by).wait_recv()
        return jnp.maximum(largest, peak_all[by])

    largest = lax.fori_loop(1, peers, take_peak, mine)
    before = scale_in[...]
    scale = largest + EPSILON * before
    scale_sent[...] = scale

    @pl.when(stage < stages - 1)
    def _():
        scale_copy.start()

    log_out[...] = jnp.log(largest / before + EPSILON)[:1]
    by_row = jnp.transpose(jnp.broadcast_to(scale[:1], (128, rows)))[:, :1]
    env_out[0] = (product[...] / by_row).astype(jnp.bfloat16)

    def drain_peak(by, carry):
        peak_copy(by).wait_send()
        return carry

    lax.fori_loop(1, peers, drain_peak, 0)

    @pl.when(stage < stages - 1)
    def _():
        scale_copy.wait_send()


def solution(mesh):
    stages, peers = mesh.shape["segment"], mesh.shape["col"]
    n = peers // 2

    def local(left_env, bit_strings, site_tensors):
        rows, width = left_env.shape
        block = block_of(rows)
        granules = rows // block
        vmem = pl.BlockSpec(memory_space=pltpu.VMEM)
        anywhere = pl.BlockSpec(memory_space=pl.ANY)
        dma = pltpu.SemaphoreType.DMA
        return pl.pallas_call(
            functools.partial(kernel, stages, peers, block),
            out_shape=(
                jax.ShapeDtypeStruct((1, rows, width), jnp.bfloat16),
                jax.ShapeDtypeStruct((1, rows), jnp.float32),
            ),
            in_specs=[anywhere, vmem, anywhere],
            out_specs=(vmem, vmem),
            scratch_shapes=[
                pltpu.VMEM((peers, 2, width, width), jnp.bfloat16),
                pltpu.VMEM((peers, rows, width), jnp.bfloat16),
                pltpu.VMEM((rows, width), jnp.float32),
                pltpu.VMEM((rows, width), jnp.bfloat16),
                pltpu.VMEM((rows, 128), jnp.float32),
                pltpu.VMEM((8, rows), jnp.float32),
                pltpu.VMEM((peers, 8, rows), jnp.float32),
                pltpu.VMEM((8, rows), jnp.float32),
                pltpu.VMEM((8, rows), jnp.float32),
                dma((2,)),
                dma((peers,)),
                dma((granules, peers)),
                dma((4, granules, n)),
                dma((granules, n)),
                dma((5, granules)),
                dma((peers,)),
                dma((peers,)),
                dma,
                dma,
                dma((5, granules)),
                dma((n,)),
                pltpu.VMEM((rows, width), jnp.bfloat16),
            ],
            compiler_params=pltpu.CompilerParams(
                collective_id=0, has_side_effects=True, vmem_limit_bytes=60 * 1024 * 1024
            ),
        )(left_env, bit_strings, site_tensors)

    return jax.shard_map(
        local,
        mesh=mesh,
        in_specs=(P(None, "col"), P(None, "segment"), P("segment", None, None, "col")),
        out_specs=(P("segment", None, "col"), P("segment", None)),
        check_vma=False,
    )
```

```python
import functools

import jax
import jax.numpy as jnp
from jax import lax
from jax.experimental import pallas as pl
from jax.experimental.pallas import tpu as pltpu
from jax.sharding import PartitionSpec as P

EPSILON = 1e-06
REACH = (0, 2, -2, 1, -1)
MESH = pl.DeviceIdType.MESH
UNIT = 16
BLOCK = 64


def block_of(rows):
    for block in range(BLOCK, 0, -UNIT):
        if rows % block == 0:
            return block
    return rows


def chip_at(step, z, n):
    low = jnp.where(step <= n - 1 - z, z + step, n - 1 - step)
    high = jnp.where(step <= z, z - step, step)
    return jnp.where(2 * z < n, low, high)


def kernel(
    stages, peers, block,
    env_in, bits_in, tensor_in, env_out, log_out,
    weights, pieces, product, outgoing, peak, peak_sent, peak_all, scale_in, scale_sent,
    load_sem, weight_sem, arrive_sem, line_sem, cross_sem, next_sem,
    peak_send_sem, peak_recv_sem, scale_send_sem, scale_recv_sem, env_sem, first_sem, env_all, bits_row, bits_all, bits_sem,
):
    rows, width = outgoing.shape
    granules = rows // block
    n = peers // 2
    stage = lax.axis_index("segment")
    me = lax.axis_index("col")
    z = me // 2
    core = me % 2

    def there(segment, col):
        return {"segment": segment, "col": col}

    load = pltpu.make_async_copy(env_in, env_all, load_sem.at[0])
    keep = pltpu.make_async_copy(env_in, pieces.at[me], load_sem.at[1])
    load.start()
    read = pltpu.make_async_copy(bits_in, bits_row, bits_sem)
    read.start()

    @pl.when(stage == 0)
    def _():
        keep.start()

    def owner_at(step):
        return chip_at(step // 2, z, n) * 2 + (core + step) % 2

    def weight_copy(owner):
        return pltpu.make_async_copy(
            tensor_in.at[0, :, pl.ds(pl.multiple_of(owner * width, width), width), :],
            weights.at[owner],
            weight_sem.at[owner],
        )

    def start_weight(step, carry):
        weight_copy(owner_at(step)).start()
        return carry

    lax.fori_loop(0, peers, start_weight, 0)

    barrier = pltpu.get_barrier_semaphore()

    def greet(by, carry):
        pl.semaphore_signal(
            barrier, inc=1, device_id=there(stage, (me + by) % peers), device_id_type=MESH
        )
        return carry

    lax.fori_loop(1, peers, greet, 0)

    def meet(turn, carry):
        segment = (stage + 1 + turn // n) % stages
        col = (z + turn) % n * 2 + core
        pl.semaphore_signal(barrier, inc=1, device_id=there(segment, col), device_id_type=MESH)
        return carry

    lax.fori_loop(0, (stages - 1) * n, meet, 0)
    pl.semaphore_wait(barrier, peers - 1 + (stages - 1) * n)

    load.wait()
    read.wait()
    bits = bits_row[...].astype(jnp.float32)
    bits_all[...] = jnp.transpose(jnp.broadcast_to(bits, (128, rows)))

    @pl.when(stage == 0)
    def _():
        keep.wait()

    def rows_of(granule):
        return pl.ds(pl.multiple_of(granule * block, block), block)

    def send(source, granule, owner, sem, segment, col):
        return pltpu.make_async_remote_copy(
            src_ref=source,
            dst_ref=pieces.at[owner, rows_of(granule), :],
            send_sem=sem,
            recv_sem=arrive_sem.at[granule, owner],
            device_id=there(segment, col),
            device_id_type=MESH,
        )

    def piece(granule, owner):
        return pieces.at[owner, rows_of(granule), :]

    def cross(granule, owner):
        sem = cross_sem.at[granule, owner // 2]
        return send(piece(granule, owner), granule, owner, sem, stage, 2 * z + 1 - core)

    end = (z == 0) | (z == n - 1)

    def spread(act, source, granule, segment, sems, slots):
        for slot in slots:
            by = REACH[slot]
            goes = (z + by >= 0) & (z + by < n)
            if by in (-1, 1):
                goes = goes & jnp.logical_not(end)

            @pl.when(goes)
            def _():
                act(send(source, granule, me, sems.at[slot, granule], segment, me + 2 * by))

    def supply_first(act):
        def supply_chip(by, carry):
            chip = (z + by) % n
            near = jnp.abs(chip - z) == 1

            @pl.when(stage == jnp.where(near, 0, 1))
            def _():
                source = env_all.at[rows_of(0), :]
                act(send(source, 0, me, first_sem.at[by], 0, chip * 2 + core))

            return carry

        lax.fori_loop(1, n, supply_chip, 0)

    def supply(act, granule):
        @pl.when(stage == jnp.minimum(granule + 1, stages - 1))
        def _():
            source = env_all.at[rows_of(granule), :]
            spread(act, source, granule, 0, env_sem, range(1, len(REACH)))

    def onward(act, granule):
        @pl.when(stage < stages - 1)
        def _():
            source = outgoing.at[rows_of(granule), :]
            spread(act, source, granule, stage + 1, next_sem, range(len(REACH)))

    def relays(granule, chip):
        needed = (stage > 0) | (granule > 0)
        return needed & (z != chip) & ((z - chip) % 2 == 0)

    def along(act, granule, chip):
        owner = chip * 2 + core
        source = piece(granule, owner)
        for slot, by in enumerate((1, -1, 2, -2)):
            goes = relays(granule, chip) & ((chip < z) if by > 0 else (chip > z))
            if by in (-1, 1):
                goes = goes | (((stage > 0) | (granule > 0)) & end & (chip == z))

            @pl.when(goes & (z + by >= 0) & (z + by < n))
            def _():
                sem = line_sem.at[slot, granule, chip]
                act(send(source, granule, owner, sem, stage, me + 2 * by))

    def start(copy):
        copy.start()

    def sent(copy):
        copy.wait_send()

    def open_granule(granule):
        @pl.when(stage > 0)
        def _():
            cross(granule, me).wait_recv()

        along(start, granule, z)
        cross(granule, me).start()

    def supply_one(granule, carry):
        supply(start, granule)
        return carry

    supply_first(start)
    lax.fori_loop(1, granules, supply_one, 0)
    chips = [chip_at(step, z, n) for step in range(n)]

    open_granule(0)

    def one_granule(granule, carry):
        here = rows_of(granule)
        bit = bits_all[here, :1] > 0.5

        def take(chip):
            cross(granule, chip * 2 + core).wait_recv()
            along(start, granule, chip)
            cross(granule, chip * 2 + core).start()

        def add(owners, first=False):
            @pl.when(granule == 0)
            def _():
                for owner in owners:
                    weight_copy(owner).wait()

            def against(which):
                total = None
                for owner in owners:
                    one = jnp.dot(
                        piece(granule, owner)[...],
                        weights[owner, which],
                        preferred_element_type=jnp.float32,
                    )
                    total = one if total is None else total + one
                return total

            part = jnp.where(bit, against(1), against(0))
            if first:
                product[here, :] = part
            else:
                product[here, :] += part

        def others(step):
            other = chips[step] * 2 + 1 - core
            cross(granule, other).wait_recv()
            return other

        for step, chip in enumerate(chips):
            own = chip * 2 + core
            last = step == n - 1
            if step > 0:

                @pl.when(relays(granule, chip))
                def _():
                    take(chip)

                if last:
                    add([others(step - 1)])

                    @pl.when(end & (granule + 1 < granules))
                    def _():
                        open_granule(granule + 1)

                @pl.when(jnp.logical_not(relays(granule, chip)))
                def _():
                    take(chip)

            if step == 0 or last:
                add([own], first=step == 0)
            else:
                add([others(step - 1), own])
        add([others(n - 1)])

        done = product[here, :]
        outgoing[here, :] = done.astype(jnp.bfloat16)
        onward(start, granule)
        largest = jnp.max(jnp.abs(done), axis=1, keepdims=True)
        peak[here, :] = jnp.broadcast_to(largest, (block, peak.shape[1]))

        @pl.when(jnp.logical_not(end) & (granule + 1 < granules))
        def _():
            open_granule(granule + 1)

        return carry

    lax.fori_loop(0, granules, one_granule, 0)

    mine = jnp.transpose(peak[...])[:8]
    peak_sent[...] = mine

    def peak_copy(by):
        return pltpu.make_async_remote_copy(
            src_ref=peak_sent,
            dst_ref=peak_all.at[by],
            send_sem=peak_send_sem.at[by],
            recv_sem=peak_recv_sem.at[by],
            device_id=there(stage, (me + by) % peers),
            device_id_type=MESH,
        )

    def start_peak(by, carry):
        peak_copy(by).start()
        return carry

    lax.fori_loop(1, peers, start_peak, 0)

    def drain(granule, carry):
        def drain_chip(chip, carry):
            along(sent, granule, chip)
            cross(granule, chip * 2 + core).wait_send()
            return carry

        lax.fori_loop(0, n, drain_chip, 0)
        onward(sent, granule)
        return carry

    lax.fori_loop(0, granules, drain, 0)

    def supplied(granule, carry):
        supply(sent, granule)
        return carry

    supply_first(sent)
    lax.fori_loop(1, granules, supplied, 0)

    scale_copy = pltpu.make_async_remote_copy(
        src_ref=scale_sent,
        dst_ref=scale_in,
        send_sem=scale_send_sem,
        recv_sem=scale_recv_sem,
        device_id=there(stage + 1, me),
        device_id_type=MESH,
    )

    @pl.when(stage == 0)
    def _():
        scale_in[...] = jnp.ones_like(scale_in)

    @pl.when(stage > 0)
    def _():
        scale_copy.wait_recv()

    def take_peak(by, largest):
        peak_copy(by).wait_recv()
        return jnp.maximum(largest, peak_all[by])

    largest = lax.fori_loop(1, peers, take_peak, mine)
    before = scale_in[...]
    scale = largest + EPSILON * before
    scale_sent[...] = scale

    @pl.when(stage < stages - 1)
    def _():
        scale_copy.start()

    log_out[...] = jnp.log(largest / before + EPSILON)[:1]
    by_row = jnp.transpose(jnp.broadcast_to(scale[:1], (128, rows)))[:, :1]
    env_out[0] = (product[...] / by_row).astype(jnp.bfloat16)

    def drain_peak(by, carry):
        peak_copy(by).wait_send()
        return carry

    lax.fori_loop(1, peers, drain_peak, 0)

    @pl.when(stage < stages - 1)
    def _():
        scale_copy.wait_send()


def solution(mesh):
    stages, peers = mesh.shape["segment"], mesh.shape["col"]
    n = peers // 2

    def local(left_env, bit_strings, site_tensors):
        rows, width = left_env.shape
        block = block_of(rows)
        granules = rows // block
        vmem = pl.BlockSpec(memory_space=pltpu.VMEM)
        anywhere = pl.BlockSpec(memory_space=pl.ANY)
        dma = pltpu.SemaphoreType.DMA
        return pl.pallas_call(
            functools.partial(kernel, stages, peers, block),
            out_shape=(
                pltpu.VMEM((1, rows, width), jnp.bfloat16),
                pltpu.VMEM((1, rows), jnp.float32),
            ),
            in_specs=[anywhere, anywhere, anywhere],
            out_specs=(vmem, vmem),
            scratch_shapes=[
                pltpu.VMEM((peers, 2, width, width), jnp.bfloat16),
                pltpu.VMEM((peers, rows, width), jnp.bfloat16),
                pltpu.VMEM((rows, width), jnp.float32),
                pltpu.VMEM((rows, width), jnp.bfloat16),
                pltpu.VMEM((rows, 128), jnp.float32),
                pltpu.VMEM((8, rows), jnp.float32),
                pltpu.VMEM((peers, 8, rows), jnp.float32),
                pltpu.VMEM((8, rows), jnp.float32),
                pltpu.VMEM((8, rows), jnp.float32),
                dma((2,)),
                dma((peers,)),
                dma((granules, peers)),
                dma((4, granules, n)),
                dma((granules, n)),
                dma((5, granules)),
                dma((peers,)),
                dma((peers,)),
                dma,
                dma,
                dma((5, granules)),
                dma((n,)),
                pltpu.VMEM((rows, width), jnp.bfloat16),
                pltpu.VMEM((1, rows), jnp.int32),
                pltpu.VMEM((rows, 128), jnp.float32),
                dma,
            ],
            compiler_params=pltpu.CompilerParams(
                collective_id=0, has_side_effects=True, vmem_limit_bytes=60 * 1024 * 1024
            ),
        )(left_env, bit_strings.reshape(1, rows), site_tensors)

    return jax.shard_map(
        local,
        mesh=mesh,
        in_specs=(P(None, "col"), P(None, "segment"), P("segment", None, None, "col")),
        out_specs=(P("segment", None, "col"), P("segment", None)),
        check_vma=False,
    )
```

```python
import functools

import jax
import jax.numpy as jnp
from jax import lax
from jax.experimental import pallas as pl
from jax.experimental.pallas import tpu as pltpu
from jax.sharding import PartitionSpec as P

EPSILON = 1e-06
REACH = (0, 2, -2, 1, -1)
MESH = pl.DeviceIdType.MESH
UNIT = 16
BLOCK = 48


def block_of(rows):
    for block in range(BLOCK, 0, -UNIT):
        if rows % block == 0:
            return block
    return rows


def chip_at(step, z, n):
    low = 2 * z < n
    start = jnp.where(low, z, n - 1 - z)
    above = n - 1 - start
    even = above // 2
    apart = jnp.where(step <= even, 2 * step, 2 * (step - even) - 1)
    apart = jnp.where(start == 0, step, apart)
    chip = jnp.where(step <= above, start + apart, n - 1 - step)
    return jnp.where(low, chip, n - 1 - chip)


def kernel(
    stages, peers, block,
    env_in, bits_in, tensor_in, env_out, log_out,
    weights, pieces, product, outgoing, peak, peak_sent, peak_all, scale_in, scale_sent,
    load_sem, weight_sem, arrive_sem, line_sem, cross_sem, next_sem,
    peak_send_sem, peak_recv_sem, scale_send_sem, scale_recv_sem, env_sem, first_sem, env_all, bits_row, bits_all, bits_sem,
):
    rows, width = outgoing.shape
    granules = rows // block
    n = peers // 2
    stage = lax.axis_index("segment")
    me = lax.axis_index("col")
    z = me // 2
    core = me % 2

    def there(segment, col):
        return {"segment": segment, "col": col}

    load = pltpu.make_async_copy(env_in, env_all, load_sem.at[0])
    keep = pltpu.make_async_copy(env_in, pieces.at[me], load_sem.at[1])
    load.start()
    read = pltpu.make_async_copy(bits_in, bits_row, bits_sem)
    read.start()

    @pl.when(stage == 0)
    def _():
        keep.start()

    def owner_at(step):
        return chip_at(step // 2, z, n) * 2 + (core + step) % 2

    def weight_copy(owner):
        return pltpu.make_async_copy(
            tensor_in.at[0, :, pl.ds(pl.multiple_of(owner * width, width), width), :],
            weights.at[owner],
            weight_sem.at[owner],
        )

    def start_weight(step, carry):
        weight_copy(owner_at(step)).start()
        return carry

    lax.fori_loop(0, peers, start_weight, 0)

    barrier = pltpu.get_barrier_semaphore()

    def greet(by, carry):
        pl.semaphore_signal(
            barrier, inc=1, device_id=there(stage, (me + by) % peers), device_id_type=MESH
        )
        return carry

    lax.fori_loop(1, peers, greet, 0)

    def meet(turn, carry):
        segment = (stage + 1 + turn // n) % stages
        col = (z + turn) % n * 2 + core
        pl.semaphore_signal(barrier, inc=1, device_id=there(segment, col), device_id_type=MESH)
        return carry

    lax.fori_loop(0, (stages - 1) * n, meet, 0)
    pl.semaphore_wait(barrier, peers - 1 + (stages - 1) * n)

    load.wait()
    read.wait()
    bits = bits_row[...].astype(jnp.float32)
    bits_all[...] = jnp.transpose(jnp.broadcast_to(bits, (128, rows)))

    @pl.when(stage == 0)
    def _():
        keep.wait()

    def rows_of(granule):
        return pl.ds(pl.multiple_of(granule * block, block), block)

    def send(source, granule, owner, sem, segment, col):
        return pltpu.make_async_remote_copy(
            src_ref=source,
            dst_ref=pieces.at[owner, rows_of(granule), :],
            send_sem=sem,
            recv_sem=arrive_sem.at[granule, owner],
            device_id=there(segment, col),
            device_id_type=MESH,
        )

    def piece(granule, owner):
        return pieces.at[owner, rows_of(granule), :]

    def cross(granule, owner):
        return send(piece(granule, owner), granule, owner, cross_sem, stage, 2 * z + 1 - core)

    end = (z == 0) | (z == n - 1)

    def spread(act, slots):
        for slot in slots:
            by = REACH[slot]
            goes = (z + by >= 0) & (z + by < n)
            if by in (-1, 1):
                goes = goes & jnp.logical_not(end)

            @pl.when(goes)
            def _():
                act(slot, me + 2 * by)

    def supply_first(act):
        def supply_chip(by, carry):
            chip = (z + by) % n
            near = jnp.abs(chip - z) == 1

            @pl.when(stage == jnp.where(near, 0, 1))
            def _():
                source = env_all.at[rows_of(0), :]
                act(send(source, 0, me, first_sem.at[by], 0, chip * 2 + core))

            return carry

        lax.fori_loop(1, n, supply_chip, 0)

    def line_of(granule):
        return min(granule + 1, stages - 1)

    def supply(granule):
        def go(slot, col):
            source = env_all.at[rows_of(granule), :]
            send(source, granule, me, env_sem.at[slot], 0, col).start()

        @pl.when(stage == jnp.minimum(granule + 1, stages - 1))
        def _():
            spread(go, range(1, len(REACH)))

    def onward(granule, slots):
        def go(slot, col):
            source = outgoing.at[rows_of(granule), :]
            send(source, granule, me, next_sem.at[slot], stage + 1, col).start()

        @pl.when(stage < stages - 1)
        def _():
            spread(go, slots)

    def relays(granule, chip):
        needed = (stage > 0) | (granule > 0)
        return needed & (z != chip) & ((z - chip) % 2 == 0)

    def along(act, granule, chip):
        for slot, by in enumerate((1, -1, 2, -2)):
            goes = relays(granule, chip) & ((chip < z) if by > 0 else (chip > z))
            if by in (-1, 1):
                goes = goes | (((stage > 0) | (granule > 0)) & end & (chip == z))

            @pl.when(goes & (z + by >= 0) & (z + by < n))
            def _():
                act(slot, me + 2 * by)

    def sent(count, sem, several=1):
        pltpu.make_async_remote_copy(
            src_ref=pieces.at[pl.ds(0, several), pl.ds(0, count), :],
            dst_ref=pieces.at[pl.ds(0, several), pl.ds(0, count), :],
            send_sem=sem,
            recv_sem=scale_recv_sem,
            device_id=there(stage, 2 * z + 1 - core),
            device_id_type=MESH,
        ).wait_send()

    def relay(granule, chip):
        owner = chip * 2 + core

        def go(slot, col):
            sem = line_sem.at[slot, chip]
            send(piece(granule, owner), granule, owner, sem, stage, col).start()

        along(go, granule, chip)

    def open_granule(granule):
        @pl.when(stage > 0)
        def _():
            cross(granule, me).wait_recv()

        relay(granule, z)
        cross(granule, me).start()

    def supply_one(granule, carry):
        supply(granule)
        return carry

    supply_first(lambda copy: copy.start())
    lax.fori_loop(1, granules, supply_one, 0)
    chips = [chip_at(step, z, n) for step in range(n)]

    open_granule(0)

    def one_granule(granule, carry):
        here = rows_of(granule)
        bit = bits_all[here, :1] > 0.5

        def take(chip):
            cross(granule, chip * 2 + core).wait_recv()
            relay(granule, chip)
            cross(granule, chip * 2 + core).start()

        def add(owners, first=False):
            @pl.when(granule == 0)
            def _():
                for owner in owners:
                    weight_copy(owner).wait()

            def against(which):
                total = None
                for owner in owners:
                    one = jnp.dot(
                        piece(granule, owner)[...],
                        weights[owner, which],
                        preferred_element_type=jnp.float32,
                    )
                    total = one if total is None else total + one
                return total

            part = jnp.where(bit, against(1), against(0))
            if first:
                product[here, :] = part
            else:
                product[here, :] += part

        def others(step):
            other = chips[step] * 2 + 1 - core
            cross(granule, other).wait_recv()
            return other

        for step, chip in enumerate(chips):
            own = chip * 2 + core
            last = step == n - 1
            if step > 0:

                @pl.when(relays(granule, chip))
                def _():
                    take(chip)

                if last:
                    add([others(step - 1)])

                    @pl.when(end & (granule + 1 < granules))
                    def _():
                        open_granule(granule + 1)

                @pl.when(jnp.logical_not(relays(granule, chip)))
                def _():
                    take(chip)

            if step == 0 or last:
                add([own], first=step == 0)
            else:
                add([others(step - 1), own])
        add([others(n - 1)])

        done = product[here, :]
        outgoing[here, :] = done.astype(jnp.bfloat16)
        onward(granule, range(len(REACH)))
        largest = jnp.max(jnp.abs(done), axis=1, keepdims=True)
        peak[here, :] = jnp.broadcast_to(largest, (block, peak.shape[1]))

        @pl.when(jnp.logical_not(end) & (granule + 1 < granules))
        def _():
            open_granule(granule + 1)

        return carry

    lax.fori_loop(0, granules, one_granule, 0)

    mine = jnp.transpose(peak[...])[:8]
    peak_sent[...] = mine

    def peak_copy(by):
        return pltpu.make_async_remote_copy(
            src_ref=peak_sent,
            dst_ref=peak_all.at[by],
            send_sem=peak_send_sem.at[by],
            recv_sem=peak_recv_sem.at[by],
            device_id=there(stage, (me + by) % peers),
            device_id_type=MESH,
        )

    def start_peak(by, carry):
        peak_copy(by).start()
        return carry

    lax.fori_loop(1, peers, start_peak, 0)

    def drain_chip(chip, carry):
        first = jnp.where(stage == 0, block, 0)
        for begins in (0, block):
            if begins < rows:

                @pl.when(first == begins)
                def _():
                    along(lambda slot, col: sent(rows - begins, line_sem.at[slot, chip]), 1, chip)

        return carry

    lax.fori_loop(0, n, drain_chip, 0)
    sent(rows, cross_sem, n)

    @pl.when(stage < stages - 1)
    def _():
        spread(lambda slot, col: sent(rows, next_sem.at[slot]), range(len(REACH)))

    for line in range(stages):
        count = sum(line_of(granule) == line for granule in range(1, granules))
        if count:

            @pl.when(stage == line)
            def _():
                spread(
                    lambda slot, col: sent(count * block, env_sem.at[slot]),
                    range(1, len(REACH)),
                )

    supply_first(lambda copy: copy.wait_send())

    scale_copy = pltpu.make_async_remote_copy(
        src_ref=scale_sent,
        dst_ref=scale_in,
        send_sem=scale_send_sem,
        recv_sem=scale_recv_sem,
        device_id=there(stage + 1, me),
        device_id_type=MESH,
    )

    @pl.when(stage == 0)
    def _():
        scale_in[...] = jnp.ones_like(scale_in)

    @pl.when(stage > 0)
    def _():
        scale_copy.wait_recv()

    def take_peak(by, largest):
        peak_copy(by).wait_recv()
        return jnp.maximum(largest, peak_all[by])

    largest = lax.fori_loop(1, peers, take_peak, mine)
    before = scale_in[...]
    scale = largest + EPSILON * before
    scale_sent[...] = scale

    @pl.when(stage < stages - 1)
    def _():
        scale_copy.start()

    log_out[...] = jnp.log(largest / before + EPSILON)[:1]
    by_row = jnp.transpose(jnp.broadcast_to(scale[:1], (128, rows)))[:, :1]
    env_out[0] = (product[...] / by_row).astype(jnp.bfloat16)

    def drain_peak(by, carry):
        peak_copy(by).wait_send()
        return carry

    lax.fori_loop(1, peers, drain_peak, 0)

    @pl.when(stage < stages - 1)
    def _():
        scale_copy.wait_send()


def solution(mesh):
    stages, peers = mesh.shape["segment"], mesh.shape["col"]
    n = peers // 2

    def local(left_env, bit_strings, site_tensors):
        rows, width = left_env.shape
        block = block_of(rows)
        granules = rows // block
        vmem = pl.BlockSpec(memory_space=pltpu.VMEM)
        anywhere = pl.BlockSpec(memory_space=pl.ANY)
        dma = pltpu.SemaphoreType.DMA
        return pl.pallas_call(
            functools.partial(kernel, stages, peers, block),
            out_shape=(
                pltpu.VMEM((1, rows, width), jnp.bfloat16),
                pltpu.VMEM((1, rows), jnp.float32),
            ),
            in_specs=[anywhere, anywhere, anywhere],
            out_specs=(vmem, vmem),
            scratch_shapes=[
                pltpu.VMEM((peers, 2, width, width), jnp.bfloat16),
                pltpu.VMEM((peers, rows, width), jnp.bfloat16),
                pltpu.VMEM((rows, width), jnp.float32),
                pltpu.VMEM((rows, width), jnp.bfloat16),
                pltpu.VMEM((rows, 128), jnp.float32),
                pltpu.VMEM((8, rows), jnp.float32),
                pltpu.VMEM((peers, 8, rows), jnp.float32),
                pltpu.VMEM((8, rows), jnp.float32),
                pltpu.VMEM((8, rows), jnp.float32),
                dma((2,)),
                dma((peers,)),
                dma((granules, peers)),
                dma((4, n)),
                dma,
                dma((5,)),
                dma((peers,)),
                dma((peers,)),
                dma,
                dma,
                dma((5,)),
                dma((n,)),
                pltpu.VMEM((rows, width), jnp.bfloat16),
                pltpu.VMEM((1, rows), jnp.int32),
                pltpu.VMEM((rows, 128), jnp.float32),
                dma,
            ],
            compiler_params=pltpu.CompilerParams(
                collective_id=0, has_side_effects=True, vmem_limit_bytes=60 * 1024 * 1024
            ),
        )(left_env, bit_strings.reshape(1, rows), site_tensors)

    return jax.shard_map(
        local,
        mesh=mesh,
        in_specs=(P(None, "col"), P(None, "segment"), P("segment", None, None, "col")),
        out_specs=(P("segment", None, "col"), P("segment", None)),
        check_vma=False,
    )
```

```python
import functools

import jax
import jax.numpy as jnp
from jax import lax
from jax.experimental import pallas as pl
from jax.experimental.pallas import tpu as pltpu
from jax.sharding import PartitionSpec as P

EPSILON = 1e-06
REACH = (0, 1, -1, 2, -2)
MESH = pl.DeviceIdType.MESH
UNIT = 16
BLOCK = 48


def block_of(rows):
    for block in range(BLOCK, 0, -UNIT):
        if rows % block == 0:
            return block
    return rows


def chip_at(step, z, n):
    low = 2 * z < n
    start = jnp.where(low, z, n - 1 - z)
    above = n - 1 - start
    even = above // 2
    apart = jnp.where(step <= even, 2 * step, 2 * (step - even) - 1)
    apart = jnp.where(start == 0, step, apart)
    chip = jnp.where(step <= above, start + apart, n - 1 - step)
    return jnp.where(low, chip, n - 1 - chip)


def kernel(
    stages, peers, block,
    env_in, bits_in, tensor_in, env_out, log_out,
    weights, pieces, product, outgoing, peak, peak_sent, peak_all, scale_in, scale_sent,
    load_sem, weight_sem, arrive_sem, line_sem, cross_sem, next_sem,
    peak_send_sem, peak_recv_sem, scale_send_sem, scale_recv_sem, env_sem, first_sem, env_all, bits_row, bits_all, bits_sem,
):
    rows, width = outgoing.shape
    granules = rows // block
    n = peers // 2
    stage = lax.axis_index("segment")
    me = lax.axis_index("col")
    z = me // 2
    core = me % 2

    def there(segment, col):
        return {"segment": segment, "col": col}

    load = pltpu.make_async_copy(env_in, env_all, load_sem.at[0])
    keep = pltpu.make_async_copy(env_in, pieces.at[me], load_sem.at[1])
    load.start()
    read = pltpu.make_async_copy(bits_in, bits_row, bits_sem)
    read.start()

    @pl.when(stage == 0)
    def _():
        keep.start()

    def owner_at(step):
        return chip_at(step // 2, z, n) * 2 + (core + step) % 2

    def weight_copy(owner):
        return pltpu.make_async_copy(
            tensor_in.at[0, :, pl.ds(pl.multiple_of(owner * width, width), width), :],
            weights.at[owner],
            weight_sem.at[owner],
        )

    def start_weight(step, carry):
        weight_copy(owner_at(step)).start()
        return carry

    lax.fori_loop(0, peers, start_weight, 0)

    barrier = pltpu.get_barrier_semaphore()

    def greet(by, carry):
        pl.semaphore_signal(
            barrier, inc=1, device_id=there(stage, (me + by) % peers), device_id_type=MESH
        )
        return carry

    lax.fori_loop(1, peers, greet, 0)

    def meet(turn, carry):
        segment = (stage + 1 + turn // n) % stages
        col = (z + turn) % n * 2 + core
        pl.semaphore_signal(barrier, inc=1, device_id=there(segment, col), device_id_type=MESH)
        return carry

    lax.fori_loop(0, (stages - 1) * n, meet, 0)
    pl.semaphore_wait(barrier, peers - 1 + (stages - 1) * n)

    load.wait()
    read.wait()
    bits = bits_row[...].astype(jnp.float32)
    bits_all[...] = jnp.transpose(jnp.broadcast_to(bits, (128, rows)))

    @pl.when(stage == 0)
    def _():
        keep.wait()

    def rows_of(granule):
        return pl.ds(pl.multiple_of(granule * block, block), block)

    def send(source, granule, owner, sem, segment, col):
        return pltpu.make_async_remote_copy(
            src_ref=source,
            dst_ref=pieces.at[owner, rows_of(granule), :],
            send_sem=sem,
            recv_sem=arrive_sem.at[granule, owner],
            device_id=there(segment, col),
            device_id_type=MESH,
        )

    def piece(granule, owner):
        return pieces.at[owner, rows_of(granule), :]

    def cross(granule, owner):
        return send(piece(granule, owner), granule, owner, cross_sem, stage, 2 * z + 1 - core)

    end = (z == 0) | (z == n - 1)

    def spread(act, slots):
        for slot in slots:
            by = REACH[slot]
            goes = (z + by >= 0) & (z + by < n)
            if by in (-1, 1):
                goes = goes & jnp.logical_not(end)

            @pl.when(goes)
            def _():
                act(slot, me + 2 * by)

    def supply_first(act):
        def supply_chip(by, carry):
            chip = (z + by) % n
            near = jnp.abs(chip - z) == 1

            @pl.when(stage == jnp.where(near, 0, 1))
            def _():
                source = env_all.at[rows_of(0), :]
                act(send(source, 0, me, first_sem.at[by], 0, chip * 2 + core))

            return carry

        lax.fori_loop(1, n, supply_chip, 0)

    def line_of(granule):
        return min(granule + 1, stages - 1)

    def supply(granule):
        def go(slot, col):
            source = env_all.at[rows_of(granule), :]
            send(source, granule, me, env_sem.at[slot], 0, col).start()

        @pl.when(stage == jnp.minimum(granule + 1, stages - 1))
        def _():
            spread(go, range(1, len(REACH)))

    def onward(granule, slots):
        def go(slot, col):
            source = outgoing.at[rows_of(granule), :]
            send(source, granule, me, next_sem.at[slot], stage + 1, col).start()

        @pl.when(stage < stages - 1)
        def _():
            spread(go, slots)

    def relays(granule, chip):
        needed = (stage > 0) | (granule > 0)
        return needed & (z != chip) & ((z - chip) % 2 == 0)

    def along(act, granule, chip):
        for slot, by in enumerate((1, -1, 2, -2)):
            goes = relays(granule, chip) & ((chip < z) if by > 0 else (chip > z))
            if by in (-1, 1):
                goes = goes | (((stage > 0) | (granule > 0)) & end & (chip == z))

            @pl.when(goes & (z + by >= 0) & (z + by < n))
            def _():
                act(slot, me + 2 * by)

    def sent(count, sem, several=1):
        pltpu.make_async_remote_copy(
            src_ref=pieces.at[pl.ds(0, several), pl.ds(0, count), :],
            dst_ref=pieces.at[pl.ds(0, several), pl.ds(0, count), :],
            send_sem=sem,
            recv_sem=scale_recv_sem,
            device_id=there(stage, 2 * z + 1 - core),
            device_id_type=MESH,
        ).wait_send()

    def relay(granule, chip):
        owner = chip * 2 + core

        def go(slot, col):
            sem = line_sem.at[slot, chip]
            send(piece(granule, owner), granule, owner, sem, stage, col).start()

        along(go, granule, chip)

    def open_granule(granule):
        @pl.when(stage > 0)
        def _():
            cross(granule, me).wait_recv()

        relay(granule, z)
        cross(granule, me).start()

    def supply_one(granule, carry):
        supply(granule)
        return carry

    supply_first(lambda copy: copy.start())
    lax.fori_loop(1, granules, supply_one, 0)
    chips = [chip_at(step, z, n) for step in range(n)]

    open_granule(0)

    def one_granule(granule, carry):
        here = rows_of(granule)
        bit = bits_all[here, :1] > 0.5

        def take(chip):
            cross(granule, chip * 2 + core).wait_recv()
            relay(granule, chip)
            cross(granule, chip * 2 + core).start()

        def add(owners, first=False):
            @pl.when(granule == 0)
            def _():
                for owner in owners:
                    weight_copy(owner).wait()

            def against(which):
                total = None
                for owner in owners:
                    one = jnp.dot(
                        piece(granule, owner)[...],
                        weights[owner, which],
                        preferred_element_type=jnp.float32,
                    )
                    total = one if total is None else total + one
                return total

            part = jnp.where(bit, against(1), against(0))
            if first:
                product[here, :] = part
            else:
                product[here, :] += part

        def others(step):
            other = chips[step] * 2 + 1 - core
            cross(granule, other).wait_recv()
            return other

        for step, chip in enumerate(chips):
            own = chip * 2 + core
            last = step == n - 1
            if step > 0:

                @pl.when(relays(granule, chip))
                def _():
                    take(chip)

                if last:
                    add([others(step - 1)])

                    @pl.when(end & (granule + 1 < granules))
                    def _():
                        open_granule(granule + 1)

                @pl.when(jnp.logical_not(relays(granule, chip)))
                def _():
                    take(chip)

            if step == 0 or last:
                add([own], first=step == 0)
            else:
                add([others(step - 1), own])
        add([others(n - 1)])

        done = product[here, :]
        outgoing[here, :] = done.astype(jnp.bfloat16)
        onward(granule, range(len(REACH)))
        largest = jnp.max(jnp.abs(done), axis=1, keepdims=True)
        peak[here, :] = jnp.broadcast_to(largest, (block, peak.shape[1]))

        @pl.when(jnp.logical_not(end) & (granule + 1 < granules))
        def _():
            open_granule(granule + 1)

        return carry

    lax.fori_loop(0, granules, one_granule, 0)

    mine = jnp.transpose(peak[...])[:8]
    peak_sent[...] = mine

    def peak_copy(by):
        return pltpu.make_async_remote_copy(
            src_ref=peak_sent,
            dst_ref=peak_all.at[by],
            send_sem=peak_send_sem.at[by],
            recv_sem=peak_recv_sem.at[by],
            device_id=there(stage, (me + by) % peers),
            device_id_type=MESH,
        )

    def start_peak(by, carry):
        peak_copy(by).start()
        return carry

    lax.fori_loop(1, peers, start_peak, 0)

    def drain_chip(chip, carry):
        first = jnp.where(stage == 0, block, 0)
        for begins in (0, block):
            if begins < rows:

                @pl.when(first == begins)
                def _():
                    along(lambda slot, col: sent(rows - begins, line_sem.at[slot, chip]), 1, chip)

        return carry

    lax.fori_loop(0, n, drain_chip, 0)
    sent(rows, cross_sem, n)

    @pl.when(stage < stages - 1)
    def _():
        spread(lambda slot, col: sent(rows, next_sem.at[slot]), range(len(REACH)))

    for line in range(stages):
        count = sum(line_of(granule) == line for granule in range(1, granules))
        if count:

            @pl.when(stage == line)
            def _():
                spread(
                    lambda slot, col: sent(count * block, env_sem.at[slot]),
                    range(1, len(REACH)),
                )

    supply_first(lambda copy: copy.wait_send())

    scale_copy = pltpu.make_async_remote_copy(
        src_ref=scale_sent,
        dst_ref=scale_in,
        send_sem=scale_send_sem,
        recv_sem=scale_recv_sem,
        device_id=there(stage + 1, me),
        device_id_type=MESH,
    )

    @pl.when(stage == 0)
    def _():
        scale_in[...] = jnp.ones_like(scale_in)

    @pl.when(stage > 0)
    def _():
        scale_copy.wait_recv()

    def take_peak(by, largest):
        peak_copy(by).wait_recv()
        return jnp.maximum(largest, peak_all[by])

    largest = lax.fori_loop(1, peers, take_peak, mine)
    before = scale_in[...]
    scale = largest + EPSILON * before
    scale_sent[...] = scale

    @pl.when(stage < stages - 1)
    def _():
        scale_copy.start()

    log_out[...] = jnp.log(largest / before + EPSILON)[:1]
    by_row = jnp.transpose(jnp.broadcast_to(scale[:1], (128, rows)))[:, :1]
    env_out[0] = (product[...] / by_row).astype(jnp.bfloat16)

    def drain_peak(by, carry):
        peak_copy(by).wait_send()
        return carry

    lax.fori_loop(1, peers, drain_peak, 0)

    @pl.when(stage < stages - 1)
    def _():
        scale_copy.wait_send()


def solution(mesh):
    stages, peers = mesh.shape["segment"], mesh.shape["col"]
    n = peers // 2

    def local(left_env, bit_strings, site_tensors):
        rows, width = left_env.shape
        block = block_of(rows)
        granules = rows // block
        vmem = pl.BlockSpec(memory_space=pltpu.VMEM)
        anywhere = pl.BlockSpec(memory_space=pl.ANY)
        dma = pltpu.SemaphoreType.DMA
        return pl.pallas_call(
            functools.partial(kernel, stages, peers, block),
            out_shape=(
                pltpu.VMEM((1, rows, width), jnp.bfloat16),
                pltpu.VMEM((1, rows), jnp.float32),
            ),
            in_specs=[anywhere, anywhere, anywhere],
            out_specs=(vmem, vmem),
            scratch_shapes=[
                pltpu.VMEM((peers, 2, width, width), jnp.bfloat16),
                pltpu.VMEM((peers, rows, width), jnp.bfloat16),
                pltpu.VMEM((rows, width), jnp.float32),
                pltpu.VMEM((rows, width), jnp.bfloat16),
                pltpu.VMEM((rows, 128), jnp.float32),
                pltpu.VMEM((8, rows), jnp.float32),
                pltpu.VMEM((peers, 8, rows), jnp.float32),
                pltpu.VMEM((8, rows), jnp.float32),
                pltpu.VMEM((8, rows), jnp.float32),
                dma((2,)),
                dma((peers,)),
                dma((granules, peers)),
                dma((4, n)),
                dma,
                dma((5,)),
                dma((peers,)),
                dma((peers,)),
                dma,
                dma,
                dma((5,)),
                dma((n,)),
                pltpu.VMEM((rows, width), jnp.bfloat16),
                pltpu.VMEM((1, rows), jnp.int32),
                pltpu.VMEM((rows, 128), jnp.float32),
                dma,
            ],
            compiler_params=pltpu.CompilerParams(
                collective_id=0, has_side_effects=True, vmem_limit_bytes=60 * 1024 * 1024
            ),
        )(left_env, bit_strings.reshape(1, rows), site_tensors)

    return jax.shard_map(
        local,
        mesh=mesh,
        in_specs=(P(None, "col"), P(None, "segment"), P("segment", None, None, "col")),
        out_specs=(P("segment", None, "col"), P("segment", None)),
        check_vma=False,
    )
```

```python
import functools

import jax
import jax.numpy as jnp
from jax import lax
from jax.experimental import pallas as pl
from jax.experimental.pallas import tpu as pltpu
from jax.sharding import PartitionSpec as P

EPSILON = 1e-06
REACH = (0, 1, -1, 2, -2)
MESH = pl.DeviceIdType.MESH
UNIT = 16
BLOCK = 48


def block_of(rows):
    for block in range(BLOCK, 0, -UNIT):
        if rows % block == 0:
            return block
    return rows


def chip_at(step, z, n):
    low = 2 * z < n
    start = jnp.where(low, z, n - 1 - z)
    above = n - 1 - start
    even = above // 2
    apart = jnp.where(step <= even, 2 * step, 2 * (step - even) - 1)
    apart = jnp.where(start == 0, step, apart)
    chip = jnp.where(step <= above, start + apart, n - 1 - step)
    return jnp.where(low, chip, n - 1 - chip)


def kernel(
    stages, peers, block,
    env_in, bits_in, tensor_in, env_out, log_out,
    weights, pieces, product, outgoing, peak, peak_sent, peak_all, scale_in, scale_sent,
    load_sem, weight_sem, arrive_sem, line_sem, cross_sem, next_sem,
    peak_send_sem, peak_recv_sem, scale_send_sem, scale_recv_sem, env_sem, first_sem, env_all, bits_row, bits_all, bits_sem,
):
    rows, width = outgoing.shape
    granules = rows // block
    n = peers // 2
    stage = lax.axis_index("segment")
    me = lax.axis_index("col")
    z = me // 2
    core = me % 2

    def there(segment, col):
        return {"segment": segment, "col": col}

    load = pltpu.make_async_copy(env_in, env_all, load_sem.at[0])
    keep = pltpu.make_async_copy(env_in, pieces.at[me], load_sem.at[1])
    load.start()
    read = pltpu.make_async_copy(bits_in, bits_row, bits_sem)
    read.start()

    @pl.when(stage == 0)
    def _():
        keep.start()

    def owner_at(step):
        return chip_at(step // 2, z, n) * 2 + (core + step) % 2

    def weight_copy(owner):
        return pltpu.make_async_copy(
            tensor_in.at[0, :, pl.ds(pl.multiple_of(owner * width, width), width), :],
            weights.at[owner],
            weight_sem.at[owner],
        )

    def start_weight(step, carry):
        weight_copy(owner_at(step)).start()
        return carry

    lax.fori_loop(0, peers, start_weight, 0)

    barrier = pltpu.get_barrier_semaphore()

    def greet(by, carry):
        pl.semaphore_signal(
            barrier, inc=1, device_id=there(stage, (me + by) % peers), device_id_type=MESH
        )
        return carry

    lax.fori_loop(1, peers, greet, 0)

    def meet(turn, carry):
        segment = (stage + 1 + turn // n) % stages
        col = (z + turn) % n * 2 + core
        pl.semaphore_signal(barrier, inc=1, device_id=there(segment, col), device_id_type=MESH)
        return carry

    lax.fori_loop(0, (stages - 1) * n, meet, 0)
    pl.semaphore_wait(barrier, peers - 1 + (stages - 1) * n)

    load.wait()
    read.wait()
    bits = bits_row[...].astype(jnp.float32)
    bits_all[...] = jnp.transpose(jnp.broadcast_to(bits, (128, rows)))

    @pl.when(stage == 0)
    def _():
        keep.wait()

    def rows_of(granule):
        return pl.ds(pl.multiple_of(granule * block, block), block)

    def send(source, granule, owner, sem, segment, col):
        return pltpu.make_async_remote_copy(
            src_ref=source,
            dst_ref=pieces.at[owner, rows_of(granule), :],
            send_sem=sem,
            recv_sem=arrive_sem.at[granule, owner],
            device_id=there(segment, col),
            device_id_type=MESH,
        )

    def piece(granule, owner):
        return pieces.at[owner, rows_of(granule), :]

    def cross(granule, owner):
        return send(piece(granule, owner), granule, owner, cross_sem, stage, 2 * z + 1 - core)

    end = (z == 0) | (z == n - 1)

    def spread(act, slots):
        for slot in slots:
            by = REACH[slot]
            goes = (z + by >= 0) & (z + by < n)
            if by in (-1, 1):
                goes = goes & jnp.logical_not(end)

            @pl.when(goes)
            def _():
                act(slot, me + 2 * by)

    def supply_first(act):
        def supply_chip(by, carry):
            chip = (z + by) % n
            near = jnp.abs(chip - z) == 1

            @pl.when(stage == jnp.where(near, 0, 1))
            def _():
                source = env_all.at[rows_of(0), :]
                act(send(source, 0, me, first_sem.at[by], 0, chip * 2 + core))

            return carry

        lax.fori_loop(1, n, supply_chip, 0)

    def line_of(granule):
        return min(granule + 1, stages - 1)

    def supply(granule):
        def go(slot, col):
            source = env_all.at[rows_of(granule), :]
            send(source, granule, me, env_sem.at[slot], 0, col).start()

        @pl.when(stage == jnp.minimum(granule + 1, stages - 1))
        def _():
            spread(go, range(1, len(REACH)))

    def onward(granule, slots):
        def go(slot, col):
            source = outgoing.at[rows_of(granule), :]
            send(source, granule, me, next_sem.at[slot], stage + 1, col).start()

        @pl.when(stage < stages - 1)
        def _():
            spread(go, slots)

    def relays(granule, chip):
        needed = (stage > 0) | (granule > 0)
        return needed & (z != chip) & ((z - chip) % 2 == 0)

    def along(act, granule, chip):
        for slot, by in enumerate((1, -1, 2, -2)):
            goes = relays(granule, chip) & ((chip < z) if by > 0 else (chip > z))
            if by in (-1, 1):
                goes = goes | (((stage > 0) | (granule > 0)) & end & (chip == z))

            @pl.when(goes & (z + by >= 0) & (z + by < n))
            def _():
                act(slot, me + 2 * by)

    def sent(count, sem, several=1):
        pltpu.make_async_remote_copy(
            src_ref=pieces.at[pl.ds(0, several), pl.ds(0, count), :],
            dst_ref=pieces.at[pl.ds(0, several), pl.ds(0, count), :],
            send_sem=sem,
            recv_sem=scale_recv_sem,
            device_id=there(stage, 2 * z + 1 - core),
            device_id_type=MESH,
        ).wait_send()

    def relay(granule, chip):
        owner = chip * 2 + core

        def go(slot, col):
            sem = line_sem.at[slot, chip]
            send(piece(granule, owner), granule, owner, sem, stage, col).start()

        along(go, granule, chip)

    def open_granule(granule):
        @pl.when(stage > 0)
        def _():
            cross(granule, me).wait_recv()

        relay(granule, z)
        cross(granule, me).start()

    def supply_one(granule, carry):
        supply(granule)
        return carry

    supply_first(lambda copy: copy.start())
    lax.fori_loop(1, granules, supply_one, 0)
    chips = [chip_at(step, z, n) for step in range(n)]

    open_granule(0)

    def one_granule(granule, carry):
        here = rows_of(granule)
        bit = bits_all[here, :1] > 0.5

        def take(chip):
            cross(granule, chip * 2 + core).wait_recv()
            relay(granule, chip)
            cross(granule, chip * 2 + core).start()

        def add(owners, first=False):
            @pl.when(granule == 0)
            def _():
                for owner in owners:
                    weight_copy(owner).wait()

            def against(which):
                total = None
                for owner in owners:
                    one = jnp.dot(
                        piece(granule, owner)[...],
                        weights[owner, which],
                        preferred_element_type=jnp.float32,
                    )
                    total = one if total is None else total + one
                return total

            part = jnp.where(bit, against(1), against(0))
            if first:
                product[here, :] = part
            else:
                product[here, :] += part

        def others(step):
            other = chips[step] * 2 + 1 - core
            cross(granule, other).wait_recv()
            return other

        for step, chip in enumerate(chips):
            own = chip * 2 + core
            last = step == n - 1
            if step > 0:

                @pl.when(relays(granule, chip))
                def _():
                    take(chip)

                if last:
                    other = others(step - 1)

                    @pl.when(end & (granule > 0) & (granule + 1 < granules))
                    def _():
                        open_granule(granule + 1)

                    add([other])

                    @pl.when(end & (granule == 0) & (granule + 1 < granules))
                    def _():
                        open_granule(granule + 1)

                @pl.when(jnp.logical_not(relays(granule, chip)))
                def _():
                    take(chip)

            if step == 0 or last:
                add([own], first=step == 0)
            else:
                add([others(step - 1), own])
        add([others(n - 1)])

        done = product[here, :]
        outgoing[here, :] = done.astype(jnp.bfloat16)
        onward(granule, range(len(REACH)))
        largest = jnp.max(jnp.abs(done), axis=1, keepdims=True)
        peak[here, :] = jnp.broadcast_to(largest, (block, peak.shape[1]))

        @pl.when(jnp.logical_not(end) & (granule + 1 < granules))
        def _():
            open_granule(granule + 1)

        return carry

    lax.fori_loop(0, granules, one_granule, 0)

    mine = jnp.transpose(peak[...])[:8]
    peak_sent[...] = mine

    def peak_copy(by):
        return pltpu.make_async_remote_copy(
            src_ref=peak_sent,
            dst_ref=peak_all.at[by],
            send_sem=peak_send_sem,
            recv_sem=peak_recv_sem.at[by],
            device_id=there(stage, (me + by) % peers),
            device_id_type=MESH,
        )

    def start_peak(by, carry):
        peak_copy(by).start()
        return carry

    lax.fori_loop(1, peers, start_peak, 0)

    def drain_chip(chip, carry):
        first = jnp.where(stage == 0, block, 0)
        for begins in (0, block):
            if begins < rows:

                @pl.when(first == begins)
                def _():
                    along(lambda slot, col: sent(rows - begins, line_sem.at[slot, chip]), 1, chip)

        return carry

    lax.fori_loop(0, n, drain_chip, 0)
    sent(rows, cross_sem, n)

    @pl.when(stage < stages - 1)
    def _():
        spread(lambda slot, col: sent(rows, next_sem.at[slot]), range(len(REACH)))

    for line in range(stages):
        count = sum(line_of(granule) == line for granule in range(1, granules))
        if count:

            @pl.when(stage == line)
            def _():
                spread(
                    lambda slot, col: sent(count * block, env_sem.at[slot]),
                    range(1, len(REACH)),
                )

    supply_first(lambda copy: copy.wait_send())

    scale_copy = pltpu.make_async_remote_copy(
        src_ref=scale_sent,
        dst_ref=scale_in,
        send_sem=scale_send_sem,
        recv_sem=scale_recv_sem,
        device_id=there(stage + 1, me),
        device_id_type=MESH,
    )

    @pl.when(stage == 0)
    def _():
        scale_in[...] = jnp.ones_like(scale_in)

    @pl.when(stage > 0)
    def _():
        scale_copy.wait_recv()

    def take_peak(by, largest):
        peak_copy(by).wait_recv()
        return jnp.maximum(largest, peak_all[by])

    largest = lax.fori_loop(1, peers, take_peak, mine)
    before = scale_in[...]
    scale = largest + EPSILON * before
    scale_sent[...] = scale

    @pl.when(stage < stages - 1)
    def _():
        scale_copy.start()

    log_out[...] = jnp.log(largest / before + EPSILON)[:1]
    by_row = jnp.transpose(jnp.broadcast_to(scale[:1], (128, rows)))[:, :1]
    env_out[0] = (product[...] / by_row).astype(jnp.bfloat16)

    pltpu.make_async_remote_copy(
        src_ref=peak_all.at[pl.ds(1, peers - 1)],
        dst_ref=peak_all.at[pl.ds(1, peers - 1)],
        send_sem=peak_send_sem,
        recv_sem=scale_recv_sem,
        device_id=there(stage, (me + 1) % peers),
        device_id_type=MESH,
    ).wait_send()

    @pl.when(stage < stages - 1)
    def _():
        scale_copy.wait_send()


def solution(mesh):
    stages, peers = mesh.shape["segment"], mesh.shape["col"]
    n = peers // 2

    def local(left_env, bit_strings, site_tensors):
        rows, width = left_env.shape
        block = block_of(rows)
        granules = rows // block
        vmem = pl.BlockSpec(memory_space=pltpu.VMEM)
        anywhere = pl.BlockSpec(memory_space=pl.ANY)
        dma = pltpu.SemaphoreType.DMA
        return pl.pallas_call(
            functools.partial(kernel, stages, peers, block),
            out_shape=(
                pltpu.VMEM((1, rows, width), jnp.bfloat16),
                pltpu.VMEM((1, rows), jnp.float32),
            ),
            in_specs=[anywhere, anywhere, anywhere],
            out_specs=(vmem, vmem),
            scratch_shapes=[
                pltpu.VMEM((peers, 2, width, width), jnp.bfloat16),
                pltpu.VMEM((peers, rows, width), jnp.bfloat16),
                pltpu.VMEM((rows, width), jnp.float32),
                pltpu.VMEM((rows, width), jnp.bfloat16),
                pltpu.VMEM((rows, 128), jnp.float32),
                pltpu.VMEM((8, rows), jnp.float32),
                pltpu.VMEM((peers, 8, rows), jnp.float32),
                pltpu.VMEM((8, rows), jnp.float32),
                pltpu.VMEM((8, rows), jnp.float32),
                dma((2,)),
                dma((peers,)),
                dma((granules, peers)),
                dma((4, n)),
                dma,
                dma((5,)),
                dma,
                dma((peers,)),
                dma,
                dma,
                dma((5,)),
                dma((n,)),
                pltpu.VMEM((rows, width), jnp.bfloat16),
                pltpu.VMEM((1, rows), jnp.int32),
                pltpu.VMEM((rows, 128), jnp.float32),
                dma,
            ],
            compiler_params=pltpu.CompilerParams(
                collective_id=0, has_side_effects=True, vmem_limit_bytes=60 * 1024 * 1024
            ),
        )(left_env, bit_strings.reshape(1, rows), site_tensors)

    return jax.shard_map(
        local,
        mesh=mesh,
        in_specs=(P(None, "col"), P(None, "segment"), P("segment", None, None, "col")),
        out_specs=(P("segment", None, "col"), P("segment", None)),
        check_vma=False,
    )
```
